32 devices in a mesh: row: 2 (over x), col: 8 (over z, y), layer: 2 (over core).
Axes of the slice: x: 2, y: 2, z: 4, core: 2. Of those that a mesh axis runs over, the one named last changes fastest.
Arguments:
- owned_blocks: bfloat16 [512, 32, 128, 128], P(('row', 'col', 'layer')), may hold values from -1 to 1
- slot_rows: int32 [512], P(('row', 'col', 'layer')), may hold values from -1 to 255, as said below
- block_cols: int32 [512, 32], P(('row', 'col', 'layer')), may hold values from 0 to 255, as said below
Outputs:
- product_blocks: bfloat16 [256, 32, 128, 128], P(('row', 'layer'), 'col')
The draws below stay inside these ranges and needn't reach their ends.
Inputs may be any that keep to these rules, and one draw needn't show every extreme that they name: `slot_rows`: every block row appears in exactly one slot. The 16 slots of the device at grid row r, grid column c and layer l (slots ((r * 8 + c) * 2 + l) * 16 onward) hold only block rows i with i // 128 = r and (i // 16) % 2 = l, or -1. In every grid row and layer some device uses all of its slots. block_cols[s, p] lies in panel p, between p * 8 and p * 8 + 7, also for unused slots.
All inputs are finite; a program needn't handle non-finite values.
Results may differ from the reference program's by a relative error of at most 0.001.
Values may be sent and summed in bfloat16 or wider, within the bound.
A program may use at most 256 MiB of HBM per device.

```python
import jax
import jax.numpy as jnp
from jax import lax

NB = 256
BLOCK_ORBITALS = 128
ROW_BLOCK_COUNT = 32
GRID_ROWS = 2
GRID_COLS = 8
LAYERS = 2
W = 8
HALF = 64
PPD = 2
OWN_CAP = 16
SLOT_COUNT = 512


def grid_order_rows_drawn():
    position = jnp.arange(NB, dtype=jnp.int32)
    group_index = position // HALF
    grid_row = group_index // LAYERS
    layer_index = group_index % LAYERS
    within = position % HALF
    upper_part = within // (PPD * W)
    inner_part = within // W % PPD
    offset = within % W
    panel_index = grid_row * (ROW_BLOCK_COUNT // GRID_ROWS) + upper_part * PPD * LAYERS + layer_index * PPD + inner_part
    return (panel_index * W + offset).astype(jnp.int32)


def local_pattern(pattern_key):
    row_index = jnp.arange(NB, dtype=jnp.int32)
    panels = jnp.arange(ROW_BLOCK_COUNT, dtype=jnp.int32)
    moves = jax.random.randint(pattern_key, (NB, ROW_BLOCK_COUNT), -1, 2, dtype=jnp.int32)
    offsets = (row_index[:, None] % W + moves) % W
    own_panel = (row_index // W)[:, None] == panels[None, :]
    offsets = jnp.where(own_panel, row_index[:, None] % W, offsets)
    return (panels[None, :] * W + offsets).astype(jnp.int32)


def one_group(group_key, group_rows):
    first_key, later_random_key, third_key = jax.random.split(group_key, 3)
    shuffled = group_rows[jax.random.permutation(first_key, HALF)]
    full_owner = jax.random.randint(later_random_key, (), 0, GRID_COLS, dtype=jnp.int32)
    others = jax.random.permutation(third_key, (GRID_COLS - 1) * OWN_CAP).astype(jnp.int32)[:HALF - OWN_CAP]
    owner_col = others // OWN_CAP
    owner_col = owner_col + (owner_col >= full_owner).astype(jnp.int32)
    slot_index = jnp.concatenate([full_owner * OWN_CAP + jnp.arange(OWN_CAP, dtype=jnp.int32), owner_col * OWN_CAP + others % OWN_CAP])
    return jnp.full((GRID_COLS * OWN_CAP,), -1, jnp.int32).at[slot_index].set(shuffled)


def owner_table(owner_key):
    grid_rows = grid_order_rows_drawn().reshape(GRID_ROWS * LAYERS, HALF)
    group_keys = jax.random.split(owner_key, GRID_ROWS * LAYERS)
    lookup_tables = jax.vmap(one_group)(group_keys, grid_rows)
    lookup_tables = lookup_tables.reshape(GRID_ROWS, LAYERS, GRID_COLS, OWN_CAP).transpose(0, 2, 1, 3)
    return lookup_tables.reshape(SLOT_COUNT)


def draw_slot_rows(key, part):
    return owner_table(jax.random.fold_in(key, 11))


def draw_block_cols(key, part):
    slot_table = owner_table(jax.random.fold_in(key, 11))
    pattern = local_pattern(jax.random.fold_in(key, 12))
    return pattern[jnp.maximum(slot_table, 0)]


def draw_owned_blocks(key, part):
    spread_scale = float(BLOCK_ORBITALS * ROW_BLOCK_COUNT) ** (-0.25)
    complete_shape = (SLOT_COUNT, ROW_BLOCK_COUNT, BLOCK_ORBITALS, BLOCK_ORBITALS)
    values = jnp.clip(jax.random.normal(key, complete_shape, jnp.float32), -4.0, 4.0)
    return (values * spread_scale).astype(jnp.bfloat16)


def setup_inputs(seed: int = 0) -> dict:
    arg_keys = jax.random.split(jax.random.key(seed), 4)
    owned_blocks = draw_owned_blocks(jax.random.fold_in(arg_keys[3], 71), 0)
    slot_rows = draw_slot_rows(jax.random.fold_in(arg_keys[3], 71), 0)
    block_cols = draw_block_cols(jax.random.fold_in(arg_keys[3], 71), 0)
    return dict(owned_blocks=owned_blocks, slot_rows=slot_rows, block_cols=block_cols)


def grid_order_rows():
    position = jnp.arange(NB, dtype=jnp.int32)
    group_index = position // HALF
    grid_row = group_index // LAYERS
    layer_index = group_index % LAYERS
    within = position % HALF
    upper_part = within // (PPD * W)
    inner_part = (within // W) % PPD
    offset = within % W
    panel_index = grid_row * (ROW_BLOCK_COUNT // GRID_ROWS) + upper_part * PPD * LAYERS + layer_index * PPD + inner_part
    return (panel_index * W + offset).astype(jnp.int32)


def reference(owned_blocks, slot_rows, block_cols):
    target = jnp.where(slot_rows >= 0, slot_rows, NB).astype(jnp.int32)
    blocks = jnp.zeros((NB, ROW_BLOCK_COUNT, BLOCK_ORBITALS, BLOCK_ORBITALS), owned_blocks.dtype).at[target].set(owned_blocks, mode="drop")
    columns = jnp.zeros((NB, ROW_BLOCK_COUNT), jnp.int32).at[target].set(block_cols.astype(jnp.int32), mode="drop")

    def one_row(row_index):
        row_columns = columns[row_index]
        left_blocks = blocks[row_index].astype(jnp.float32)
        partner = blocks[row_columns].astype(jnp.float32)
        partner_cols = columns[row_columns]
        matched = (partner_cols == row_columns[None, :]).astype(jnp.float32)
        partner = partner * matched[:, :, None, None]
        summed = jnp.einsum("tab,tsbc->sac", left_blocks, partner)
        return summed.astype(jnp.bfloat16)

    grid_order = grid_order_rows()
    return lax.map(one_row, grid_order)
```

```python
import functools

import jax
import jax.numpy as jnp
from jax import lax
from jax.experimental import pallas as pl
from jax.experimental.pallas import tpu as pltpu
from jax.sharding import PartitionSpec as P

MESH = pl.DeviceIdType.MESH
QUAD = 4


def pick_kernel(index_ref, got_ref, tile_ref, sems):
    count = tile_ref.shape[0]

    def copy(place):
        return pltpu.make_async_copy(
            got_ref.at[index_ref[place]], tile_ref.at[place], sems.at[place]
        )

    @pl.loop(0, count)
    def _(place):
        copy(place).start()

    @pl.loop(0, count)
    def _(place):
        copy(place).wait()


def pick_rows(index, got):
    count = index.shape[0]
    return pl.pallas_call(
        pick_kernel,
        out_shape=jax.ShapeDtypeStruct((count,) + got.shape[1:], got.dtype),
        in_specs=[
            pl.BlockSpec(memory_space=pltpu.SMEM),
            pl.BlockSpec(memory_space=pl.ANY),
        ],
        out_specs=pl.BlockSpec(memory_space=pl.ANY),
        scratch_shapes=[pltpu.SemaphoreType.DMA((count,))],
        name="pick_rows",
    )(index, got)


def spread_kernel(
    rows, cols, layers, outer, swapped, tile_ref, left_ref, right_ref,
    local_sem, send_sem, recv_sem, row_send, layer_send, table_recv,
):
    inner = cols // outer
    my_row, my_col, my_layer = (lax.axis_index(a) for a in ("row", "col", "layer"))
    my_outer, my_inner = my_col // inner, lax.rem(my_col, inner)
    my_group = my_row * layers + my_layer
    height = tile_ref.shape[0]

    barrier = pltpu.get_barrier_semaphore()
    lines = (
        (my_outer + 1 < outer, {"col": my_col + inner}),
        (my_outer >= 1, {"col": my_col - inner}),
        (my_inner + 1 < inner, {"col": my_col + 1}),
        (my_inner >= 1, {"col": my_col - 1}),
    )
    met = jnp.int32(rows - 1 + layers - 1)
    for there, device in lines:
        met = met + there.astype(jnp.int32)

        @pl.when(there)
        def _(device=device):
            pl.semaphore_signal(barrier, inc=1, device_id=device, device_id_type=MESH)

    row_peers = [lax.rem(my_row + d, rows) for d in range(1, rows)]
    layer_peers = [lax.rem(my_layer + d, layers) for d in range(1, layers)]
    for peer in row_peers:
        pl.semaphore_signal(barrier, inc=1, device_id={"row": peer}, device_id_type=MESH)
    for peer in layer_peers:
        pl.semaphore_signal(barrier, inc=1, device_id={"layer": peer}, device_id_type=MESH)
    pl.semaphore_wait(barrier, met)

    ending = []

    def send_left(kind, part, item, way, condition, own):
        def make():
            place = left_ref.at[item, part]
            return pltpu.make_async_remote_copy(
                src_ref=tile_ref.at[part] if own else place,
                dst_ref=place,
                send_sem=send_sem.at[kind, item, way],
                recv_sem=recv_sem.at[kind, item],
                device_id=lines[way][1],
                device_id_type=MESH,
            )

        condition = jnp.logical_and(condition, lines[way][0])

        @pl.when(condition)
        def _():
            make().start()

        ending.append((condition, make))

    def wait_left(kind, part, item, condition):
        @pl.when(condition)
        def _():
            place = left_ref.at[item, part]
            pltpu.make_async_remote_copy(
                src_ref=place,
                dst_ref=place,
                send_sem=send_sem.at[kind, item, 0],
                recv_sem=recv_sem.at[kind, item],
                device_id={"col": my_col},
                device_id_type=MESH,
            ).wait_recv()

    always = my_col >= 0
    axes = (
        (outer, inner, my_outer, (0, 1)),
        (inner, 1, my_inner, (2, 3)),
    )

    def stages(kind, part, first, second):
        size1, stride1, me1, ways1 = first
        size2, stride2, me2, ways2 = second

        def own():
            for way in ways1 + ways2:
                send_left(kind, part, my_col, way, always, True)

        def along_first(step):
            for sign, way in ((-1, ways1[0]), (1, ways1[1])):
                at = me1 + sign * step
                there = at >= 0 if sign < 0 else at < size1
                item = at * stride1 + me2 * stride2
                wait_left(kind, part, item, there)
                for onward in (way,) + ways2:
                    send_left(kind, part, item, onward, there, False)

        def along_second(step):
            for sign, way in ((-1, ways2[0]), (1, ways2[1])):
                at = me2 + sign * step
                there = at >= 0 if sign < 0 else at < size2
                for other in range(size1):
                    item = other * stride1 + at * stride2
                    wait_left(kind, part, item, there)
                    send_left(kind, part, item, way, there, False)

        return (
            [own]
            + [functools.partial(along_first, s) for s in range(1, size1)]
            + [functools.partial(along_second, s) for s in range(1, size2)]
        )

    main = stages(0, pl.ds(0, height - swapped), axes[0], axes[1])
    side = stages(1, pl.ds(height - swapped, swapped), axes[1], axes[0])

    def row_copy(d, peer):
        return pltpu.make_async_remote_copy(
            src_ref=tile_ref,
            dst_ref=right_ref.at[my_group],
            send_sem=row_send.at[d],
            recv_sem=table_recv.at[my_group],
            device_id={"row": peer},
            device_id_type=MESH,
        )

    def layer_copy(d, peer, row, own):
        group = row * layers + my_layer
        return pltpu.make_async_remote_copy(
            src_ref=tile_ref if own else right_ref.at[group],
            dst_ref=right_ref.at[group],
            send_sem=layer_send.at[d, row],
            recv_sem=table_recv.at[group],
            device_id={"layer": peer},
            device_id_type=MESH,
        )

    def wait_table(group):
        pltpu.make_async_remote_copy(
            src_ref=right_ref.at[group],
            dst_ref=right_ref.at[group],
            send_sem=row_send.at[0],
            recv_sem=table_recv.at[group],
            device_id={"row": my_row},
            device_id_type=MESH,
        ).wait_recv()

    side[0]()
    main[0]()
    for d, peer in enumerate(row_peers):
        row_copy(d, peer).start()
    for d, peer in enumerate(layer_peers):
        layer_copy(d, peer, my_row, True).start()
    locals_ = (
        pltpu.make_async_copy(tile_ref, left_ref.at[my_col], local_sem.at[0]),
        pltpu.make_async_copy(tile_ref, right_ref.at[my_group], local_sem.at[1]),
    )
    for copy in locals_:
        copy.start()
    side[1]()
    rest = side[2:]
    for index, stage in enumerate(main[1:]):
        stage()
        if index < len(rest):
            rest[index]()
        if index == 0:
            for peer in row_peers:
                wait_table(peer * layers + my_layer)
                for d, layer_peer in enumerate(layer_peers):
                    layer_copy(d, layer_peer, peer, False).start()
    for stage in rest[len(main) - 1:]:
        stage()
    for layer_peer in layer_peers:
        for row in range(rows):
            wait_table(row * layers + layer_peer)
    for copy in locals_:
        copy.wait()
    for condition, make in ending:

        @pl.when(condition)
        def _(make=make):
            make().wait_send()

    for d, peer in enumerate(row_peers):
        row_copy(d, peer).wait_send()
    for d, peer in enumerate(layer_peers):
        for row in [my_row] + row_peers:
            layer_copy(d, peer, row, True).wait_send()


def spread(tile, rows, cols, layers):
    outer = 4 if cols % 4 == 0 else 1
    swapped = max(tile.shape[0] // 8, 1)
    return pl.pallas_call(
        functools.partial(spread_kernel, rows, cols, layers, outer, swapped),
        out_shape=(
            jax.ShapeDtypeStruct((cols,) + tile.shape, tile.dtype),
            jax.ShapeDtypeStruct((rows * layers,) + tile.shape, tile.dtype),
        ),
        in_specs=[pl.BlockSpec(memory_space=pl.ANY)],
        out_specs=(pl.BlockSpec(memory_space=pl.ANY), pl.BlockSpec(memory_space=pl.ANY)),
        scratch_shapes=[
            pltpu.SemaphoreType.DMA((2,)),
            pltpu.SemaphoreType.DMA((2, cols, 4)),
            pltpu.SemaphoreType.DMA((2, cols)),
            pltpu.SemaphoreType.DMA((rows,)),
            pltpu.SemaphoreType.DMA((layers, rows)),
            pltpu.SemaphoreType.DMA((rows * layers,)),
        ],
        compiler_params=pltpu.CompilerParams(collective_id=0, has_side_effects=True),
        name="spread",
    )(tile)


def multiply_kernel(pair_ref, turns_ref, left_ref, right_hbm, out_ref, table, sem):
    row = pl.program_id(0)
    nb = right_hbm.shape[0]
    width = out_ref.shape[1]
    panels = left_ref.shape[0] * left_ref.shape[2]

    @pl.when(row == 0)
    def _():
        copy = pltpu.make_async_copy(right_hbm, table.at[pl.ds(0, nb)], sem)
        copy.start()
        table[nb] = jnp.zeros_like(table[nb])
        copy.wait()

    group = 2 if width % 2 == 0 else 1
    for base in range(0, width, group):

        def step(turn, sums, base=base):
            new = []
            for j in range(group):
                start = (row * width + base + j) * panels + turn * QUAD
                lefts, rights = [], []
                for q in range(QUAD):
                    code = pair_ref[start + q]
                    panel, place = code // 1024, lax.rem(code, 1024)
                    lefts.append(left_ref[panel // width, 0, lax.rem(panel, width)])
                    rights.append(table[place, base + j])
                new.append(
                    sums[j]
                    + jnp.dot(
                        jnp.concatenate(lefts, axis=1),
                        jnp.concatenate(rights, axis=0),
                        preferred_element_type=jnp.float32,
                    )
                )
            return tuple(new)

        zero = jnp.zeros(out_ref.shape[2:], jnp.float32)
        turns = turns_ref[row * width + base]
        for j in range(1, group):
            turns = jnp.maximum(turns, turns_ref[row * width + base + j])
        sums = lax.fori_loop(0, turns, step, (zero,) * group)
        for j in range(group):
            out_ref[0, base + j] = sums[j].astype(out_ref.dtype)


def multiply(pairs, turns, left, right):
    cols, height, width, size, _ = left.shape
    nb = right.shape[0]
    table_bytes = (nb + 1) * width * size * size * 2
    return pl.pallas_call(
        multiply_kernel,
        out_shape=jax.ShapeDtypeStruct((height, width, size, size), left.dtype),
        grid_spec=pltpu.PrefetchScalarGridSpec(
            num_scalar_prefetch=2,
            grid=(height,),
            in_specs=[
                pl.BlockSpec((cols, 1, width, size, size), lambda i, *_: (0, i, 0, 0, 0)),
                pl.BlockSpec(memory_space=pl.ANY),
            ],
            out_specs=pl.BlockSpec((1, width, size, size), lambda i, *_: (i, 0, 0, 0)),
            scratch_shapes=[
                pltpu.VMEM((nb + 1, width, size, size), left.dtype),
                pltpu.SemaphoreType.DMA,
            ],
        ),
        compiler_params=pltpu.CompilerParams(vmem_limit_bytes=table_bytes + (10 << 20)),
        name="multiply",
    )(pairs, turns, left, right)


def shards(owned_blocks, slot_rows, block_cols):
    own_slots, panels, size, _ = owned_blocks.shape
    rows = lax.axis_size("row")
    cols = lax.axis_size("col")
    layers = lax.axis_size("layer")
    width = panels // cols
    slots = own_slots * rows * cols * layers
    my_row, my_col, my_layer = (lax.axis_index(a) for a in ("row", "col", "layer"))
    my_group = my_row * layers + my_layer

    got = lax.all_to_all(
        owned_blocks.reshape(own_slots, cols, width, size, size),
        "col", split_axis=1, concat_axis=0, tiled=True,
    ).reshape(cols * own_slots, width, size, size)

    ids = jnp.concatenate([slot_rows[:, None], block_cols], axis=1)
    ids = lax.all_gather(ids, ("row", "col", "layer"), axis=0, tiled=True)
    nb = NB
    per_layer = panels // (cols * layers) * (nb // panels)
    height = nb // (rows * layers)
    place = jnp.arange(nb, dtype=jnp.int32)
    part, within = place // height, place % height
    row_at = (
        part // layers * (nb // rows)
        + within // per_layer * per_layer * layers
        + part % layers * per_layer
        + within % per_layer
    )
    holds = ids[None, :, 0] == row_at[:, None]
    slot_at = jnp.sum(
        jnp.where(holds, jnp.arange(slots, dtype=jnp.int32)[None, :], 0), axis=1
    )
    my_slots = lax.dynamic_slice_in_dim(slot_at, my_group * height, height)
    owner = my_slots // own_slots // layers % cols
    tile = pick_rows(owner * own_slots + my_slots % own_slots, got)
    left, right = spread(tile, rows, cols, layers)

    columns = ids[slot_at, 1:]
    place_of = jnp.sum(
        jnp.where(row_at[:, None] == place[None, :], place[:, None], 0), axis=0
    )
    mine = lax.dynamic_slice_in_dim(columns, my_group * height, height)
    wanted = lax.dynamic_slice_in_dim(mine, my_col * width, width, 1)
    partner = place_of[mine]
    reach = lax.dynamic_slice_in_dim(columns, my_col * width, width, 1)
    matched = reach[partner] == wanted[:, None, :]
    matched = matched.transpose(0, 2, 1)
    order = jnp.cumsum(matched.astype(jnp.int32), axis=2) - 1
    code = jnp.arange(panels, dtype=jnp.int32)[None, :] * 1024 + partner
    lane = jnp.arange(panels, dtype=jnp.int32)
    taken = matched[..., None] & (order[..., None] == lane)
    pairs = jnp.sum(jnp.where(taken, (code - nb)[:, None, :, None], 0), axis=2) + nb
    turns = (jnp.sum(matched, axis=2, dtype=jnp.int32) + QUAD - 1) // QUAD
    return multiply(
        pairs.reshape(-1), turns.reshape(-1), left, right.reshape(nb, width, size, size)
    )


NB = 256


def solution(mesh):
    return jax.shard_map(
        shards,
        mesh=mesh,
        in_specs=(
            P(("row", "col", "layer"), None, None, None),
            P(("row", "col", "layer")),
            P(("row", "col", "layer"), None),
        ),
        out_specs=P(("row", "layer"), "col", None, None),
        check_vma=False,
    )
```

```python
import functools

import jax
import jax.numpy as jnp
from jax import lax
from jax.experimental import pallas as pl
from jax.experimental.pallas import tpu as pltpu
from jax.sharding import PartitionSpec as P

MESH = pl.DeviceIdType.MESH
QUAD = 4


def pick_kernel(index_ref, spot_ref, got_ref, left_ref, right_ref):
    block = got_ref[0]
    left_ref[0, 0] = block
    right_ref[0, 0] = block


def pick_rows(index, spot, got, cols, groups):
    height = index.shape[0]
    block = got.shape[1:]
    return pl.pallas_call(
        pick_kernel,
        out_shape=(
            jax.ShapeDtypeStruct((cols, height) + block, got.dtype),
            jax.ShapeDtypeStruct((groups, height) + block, got.dtype),
        ),
        grid_spec=pltpu.PrefetchScalarGridSpec(
            num_scalar_prefetch=2,
            grid=(height,),
            in_specs=[
                pl.BlockSpec((1,) + block, lambda i, index, spot: (index[i], 0, 0, 0)),
            ],
            out_specs=(
                pl.BlockSpec((1, 1) + block, lambda i, index, spot: (spot[0], i, 0, 0, 0)),
                pl.BlockSpec((1, 1) + block, lambda i, index, spot: (spot[1], i, 0, 0, 0)),
            ),
        ),
        name="pick_rows",
    )(index, spot, got)


def spread_kernel(
    rows, cols, layers, outer, parts, left_in, right_in, left_ref, right_ref,
    send_sem, recv_sem, row_send, layer_send, table_recv,
):
    inner = cols // outer
    my_row, my_col, my_layer = (lax.axis_index(a) for a in ("row", "col", "layer"))
    my_outer, my_inner = my_col // inner, lax.rem(my_col, inner)
    my_group = my_row * layers + my_layer

    barrier = pltpu.get_barrier_semaphore()
    lines = (
        (my_outer + 1 < outer, {"col": my_col + inner}),
        (my_outer >= 1, {"col": my_col - inner}),
        (my_inner + 1 < inner, {"col": my_col + 1}),
        (my_inner >= 1, {"col": my_col - 1}),
    )
    met = jnp.int32(rows - 1 + layers - 1)
    for there, device in lines:
        met = met + there.astype(jnp.int32)

        @pl.when(there)
        def _(device=device):
            pl.semaphore_signal(barrier, inc=1, device_id=device, device_id_type=MESH)

    row_peers = [lax.rem(my_row + d, rows) for d in range(1, rows)]
    layer_peers = [lax.rem(my_layer + d, layers) for d in range(1, layers)]
    for peer in row_peers:
        pl.semaphore_signal(barrier, inc=1, device_id={"row": peer}, device_id_type=MESH)
    for peer in layer_peers:
        pl.semaphore_signal(barrier, inc=1, device_id={"layer": peer}, device_id_type=MESH)
    pl.semaphore_wait(barrier, met)

    ending = []

    def send_left(kind, part, item, way, condition):
        def make():
            place = left_ref.at[item, part]
            return pltpu.make_async_remote_copy(
                src_ref=place,
                dst_ref=place,
                send_sem=send_sem.at[kind, item, way],
                recv_sem=recv_sem.at[kind, item],
                device_id=lines[way][1],
                device_id_type=MESH,
            )

        condition = jnp.logical_and(condition, lines[way][0])

        @pl.when(condition)
        def _():
            make().start()

        ending.append((condition, make))

    def wait_left(kind, part, item, condition):
        @pl.when(condition)
        def _():
            place = left_ref.at[item, part]
            pltpu.make_async_remote_copy(
                src_ref=place,
                dst_ref=place,
                send_sem=send_sem.at[kind, item, 0],
                recv_sem=recv_sem.at[kind, item],
                device_id={"col": my_col},
                device_id_type=MESH,
            ).wait_recv()

    always = my_col >= 0
    axes = (
        (outer, inner, my_outer, (0, 1)),
        (inner, 1, my_inner, (2, 3)),
    )

    def stages(kind, part, first, second):
        size1, stride1, me1, ways1 = first
        size2, stride2, me2, ways2 = second

        def own():
            for way in ways1 + ways2:
                send_left(kind, part, my_col, way, always)

        def along_first(step):
            for sign, way in ((-1, ways1[0]), (1, ways1[1])):
                at = me1 + sign * step
                there = at >= 0 if sign < 0 else at < size1
                item = at * stride1 + me2 * stride2
                wait_left(kind, part, item, there)
                for onward in (way,) + ways2:
                    send_left(kind, part, item, onward, there)

        def along_second(step):
            for sign, way in ((-1, ways2[0]), (1, ways2[1])):
                at = me2 + sign * step
                there = at >= 0 if sign < 0 else at < size2
                for other in range(size1):
                    item = other * stride1 + at * stride2
                    wait_left(kind, part, item, there)
                    send_left(kind, part, item, way, there)

        return (
            [own]
            + [functools.partial(along_first, s) for s in range(1, size1)]
            + [functools.partial(along_second, s) for s in range(1, size2)]
        )

    plans = [
        stages(kind, pl.ds(start, size), *(axes if straight else axes[::-1]))
        for kind, (start, size, straight) in enumerate(parts)
    ]

    def row_copy(d, peer):
        return pltpu.make_async_remote_copy(
            src_ref=right_ref.at[my_group],
            dst_ref=right_ref.at[my_group],
            send_sem=row_send.at[d],
            recv_sem=table_recv.at[my_group],
            device_id={"row": peer},
            device_id_type=MESH,
        )

    def layer_copy(d, peer, row):
        group = row * layers + my_layer
        return pltpu.make_async_remote_copy(
            src_ref=right_ref.at[group],
            dst_ref=right_ref.at[group],
            send_sem=layer_send.at[d, row],
            recv_sem=table_recv.at[group],
            device_id={"layer": peer},
            device_id_type=MESH,
        )

    def wait_table(group):
        pltpu.make_async_remote_copy(
            src_ref=right_ref.at[group],
            dst_ref=right_ref.at[group],
            send_sem=row_send.at[0],
            recv_sem=table_recv.at[group],
            device_id={"row": my_row},
            device_id_type=MESH,
        ).wait_recv()

    for plan in plans:
        plan[0]()
    for d, peer in enumerate(row_peers):
        row_copy(d, peer).start()
    for d, peer in enumerate(layer_peers):
        layer_copy(d, peer, my_row).start()
    for index in range(1, len(plans[0])):
        for plan in plans:
            plan[index]()
        if index == 1:
            for peer in row_peers:
                wait_table(peer * layers + my_layer)
                for d, layer_peer in enumerate(layer_peers):
                    layer_copy(d, layer_peer, peer).start()
    for layer_peer in layer_peers:
        for row in range(rows):
            wait_table(row * layers + layer_peer)
    for condition, make in ending:

        @pl.when(condition)
        def _(make=make):
            make().wait_send()

    for d, peer in enumerate(row_peers):
        row_copy(d, peer).wait_send()
    for d, peer in enumerate(layer_peers):
        for row in [my_row] + row_peers:
            layer_copy(d, peer, row).wait_send()


def spread(left, right, rows, cols, layers):
    outer = 4 if cols % 4 == 0 else 1
    height = left.shape[1]
    swapped = max(height // 8, 1)
    count = min(4, height - swapped)
    cuts = [swapped + (height - swapped) * k // count for k in range(count + 1)]
    parts = [(0, swapped, False)]
    parts += [(lo, hi - lo, True) for lo, hi in zip(cuts, cuts[1:])]
    kinds = len(parts)
    return pl.pallas_call(
        functools.partial(spread_kernel, rows, cols, layers, outer, tuple(parts)),
        out_shape=(
            jax.ShapeDtypeStruct(left.shape, left.dtype),
            jax.ShapeDtypeStruct(right.shape, right.dtype),
        ),
        in_specs=[pl.BlockSpec(memory_space=pl.ANY), pl.BlockSpec(memory_space=pl.ANY)],
        out_specs=(pl.BlockSpec(memory_space=pl.ANY), pl.BlockSpec(memory_space=pl.ANY)),
        input_output_aliases={0: 0, 1: 1},
        scratch_shapes=[
            pltpu.SemaphoreType.DMA((kinds, cols, 4)),
            pltpu.SemaphoreType.DMA((kinds, cols)),
            pltpu.SemaphoreType.DMA((rows,)),
            pltpu.SemaphoreType.DMA((layers, rows)),
            pltpu.SemaphoreType.DMA((rows * layers,)),
        ],
        compiler_params=pltpu.CompilerParams(collective_id=0, has_side_effects=True),
        name="spread",
    )(left, right)


def multiply_kernel(pair_ref, turns_ref, left_ref, right_hbm, out_ref, table, sem):
    row = pl.program_id(0)
    nb = right_hbm.shape[0]
    width = out_ref.shape[1]
    panels = left_ref.shape[0] * left_ref.shape[2]

    @pl.when(row == 0)
    def _():
        copy = pltpu.make_async_copy(right_hbm, table.at[pl.ds(0, nb)], sem)
        copy.start()
        table[nb] = jnp.zeros_like(table[nb])
        copy.wait()

    group = 2 if width % 2 == 0 else 1
    for base in range(0, width, group):

        def step(turn, sums, base=base):
            new = []
            for j in range(group):
                start = (row * width + base + j) * panels + turn * QUAD
                lefts, rights = [], []
                for q in range(QUAD):
                    code = pair_ref[start + q]
                    panel, place = code // 1024, lax.rem(code, 1024)
                    lefts.append(left_ref[panel // width, 0, lax.rem(panel, width)])
                    rights.append(table[place, base + j])
                new.append(
                    sums[j]
                    + jnp.dot(
                        jnp.concatenate(lefts, axis=1),
                        jnp.concatenate(rights, axis=0),
                        preferred_element_type=jnp.float32,
                    )
                )
            return tuple(new)

        zero = jnp.zeros(out_ref.shape[2:], jnp.float32)
        turns = turns_ref[row * width + base]
        for j in range(1, group):
            turns = jnp.maximum(turns, turns_ref[row * width + base + j])
        sums = lax.fori_loop(0, turns, step, (zero,) * group)
        for j in range(group):
            out_ref[0, base + j] = sums[j].astype(out_ref.dtype)


def multiply(pairs, turns, left, right):
    cols, height, width, size, _ = left.shape
    nb = right.shape[0]
    table_bytes = (nb + 1) * width * size * size * 2
    return pl.pallas_call(
        multiply_kernel,
        out_shape=jax.ShapeDtypeStruct((height, width, size, size), left.dtype),
        grid_spec=pltpu.PrefetchScalarGridSpec(
            num_scalar_prefetch=2,
            grid=(height,),
            in_specs=[
                pl.BlockSpec((cols, 1, width, size, size), lambda i, *_: (0, i, 0, 0, 0)),
                pl.BlockSpec(memory_space=pl.ANY),
            ],
            out_specs=pl.BlockSpec((1, width, size, size), lambda i, *_: (i, 0, 0, 0)),
            scratch_shapes=[
                pltpu.VMEM((nb + 1, width, size, size), left.dtype),
                pltpu.SemaphoreType.DMA,
            ],
        ),
        compiler_params=pltpu.CompilerParams(vmem_limit_bytes=table_bytes + (10 << 20)),
        name="multiply",
    )(pairs, turns, left, right)


def shards(owned_blocks, slot_rows, block_cols):
    own_slots, panels, size, _ = owned_blocks.shape
    rows = lax.axis_size("row")
    cols = lax.axis_size("col")
    layers = lax.axis_size("layer")
    width = panels // cols
    slots = own_slots * rows * cols * layers
    my_row, my_col, my_layer = (lax.axis_index(a) for a in ("row", "col", "layer"))
    my_group = my_row * layers + my_layer

    ids = jnp.concatenate([slot_rows[:, None], block_cols], axis=1)
    ids = lax.all_gather(ids, ("row", "col", "layer"), axis=0, tiled=True)
    owned_blocks, ids = lax.optimization_barrier((owned_blocks, ids))
    got = lax.all_to_all(
        owned_blocks.reshape(own_slots, cols, width, size, size),
        "col", split_axis=1, concat_axis=0, tiled=True,
    ).reshape(cols * own_slots, width, size, size)

    nb = NB
    per_layer = panels // (cols * layers) * (nb // panels)
    height = nb // (rows * layers)
    place = jnp.arange(nb, dtype=jnp.int32)
    part, within = place // height, place % height
    row_at = (
        part // layers * (nb // rows)
        + within // per_layer * per_layer * layers
        + part % layers * per_layer
        + within % per_layer
    )
    holds = ids[None, :, 0] == row_at[:, None]
    slot_at = jnp.sum(
        jnp.where(holds, jnp.arange(slots, dtype=jnp.int32)[None, :], 0), axis=1
    )
    my_slots = lax.dynamic_slice_in_dim(slot_at, my_group * height, height)
    owner = my_slots // own_slots // layers % cols
    left, right = pick_rows(
        owner * own_slots + my_slots % own_slots,
        jnp.stack([my_col, my_group]).astype(jnp.int32),
        got, cols, rows * layers,
    )
    left, right = spread(left, right, rows, cols, layers)

    columns = jnp.dot(
        holds.astype(jnp.float32),
        ids[:, 1:].astype(jnp.float32),
        precision=lax.Precision.HIGHEST,
    ).astype(jnp.int32)
    mine = lax.dynamic_slice_in_dim(columns, my_group * height, height)
    wanted = lax.dynamic_slice_in_dim(mine, my_col * width, width, 1)
    inside = mine % (nb // rows)
    partner = (
        (mine // (nb // rows) * layers + inside // per_layer % layers) * height
        + inside // (per_layer * layers) * per_layer
        + inside % per_layer
    )
    reach = lax.dynamic_slice_in_dim(columns, my_col * width, width, 1)
    matched = reach[partner] == wanted[:, None, :]
    matched = matched.transpose(0, 2, 1)
    order = jnp.cumsum(matched.astype(jnp.int32), axis=2) - 1
    code = jnp.arange(panels, dtype=jnp.int32)[None, :] * 1024 + partner
    lane = jnp.arange(panels, dtype=jnp.int32)
    taken = matched[..., None] & (order[..., None] == lane)
    pairs = jnp.sum(jnp.where(taken, (code - nb)[:, None, :, None], 0), axis=2) + nb
    turns = (jnp.sum(matched, axis=2, dtype=jnp.int32) + QUAD - 1) // QUAD
    return multiply(
        pairs.reshape(-1), turns.reshape(-1), left, right.reshape(nb, width, size, size)
    )


NB = 256


def solution(mesh):
    return jax.shard_map(
        shards,
        mesh=mesh,
        in_specs=(
            P(("row", "col", "layer"), None, None, None),
            P(("row", "col", "layer")),
            P(("row", "col", "layer"), None),
        ),
        out_specs=P(("row", "layer"), "col", None, None),
        check_vma=False,
    )
```

```python
import functools

import jax
import jax.numpy as jnp
from jax import lax
from jax.experimental import pallas as pl
from jax.experimental.pallas import tpu as pltpu
from jax.sharding import PartitionSpec as P

MESH = pl.DeviceIdType.MESH
QUAD = 4


def pick_kernel(index_ref, spot_ref, got_ref, *refs):
    left_ref, right_ref = refs[-2:]
    block = got_ref[0]
    left_ref[0, 0] = block
    right_ref[0, 0] = block


def pick_rows(index, spot, got, shapes, half, tables):
    height = index.shape[0]
    block = got.shape[1:]
    anywhere = pl.BlockSpec(memory_space=pl.ANY)
    return pl.pallas_call(
        pick_kernel,
        out_shape=shapes,
        grid_spec=pltpu.PrefetchScalarGridSpec(
            num_scalar_prefetch=2,
            grid=(height,),
            in_specs=[
                pl.BlockSpec((1,) + block, lambda i, index, spot: (index[i], 0, 0, 0)),
            ] + [anywhere] * len(tables),
            out_specs=(
                pl.BlockSpec((1, 1) + block, lambda i, index, spot: (spot[0], i, half, 0, 0)),
                pl.BlockSpec((1, 1) + block, lambda i, index, spot: (spot[1], i, half, 0, 0)),
            ),
        ),
        input_output_aliases={3: 0, 4: 1} if tables else {},
        name="pick_rows",
    )(index, spot, got, *tables)


def spread_kernel(
    rows, cols, layers, outer, parts, panels, left_in, right_in, left_ref, right_ref,
    send_sem, recv_sem, row_send, layer_send, table_recv,
):
    inner = cols // outer
    my_row, my_col, my_layer = (lax.axis_index(a) for a in ("row", "col", "layer"))
    my_outer, my_inner = my_col // inner, lax.rem(my_col, inner)
    my_group = my_row * layers + my_layer

    barrier = pltpu.get_barrier_semaphore()
    lines = (
        (my_outer + 1 < outer, {"col": my_col + inner}),
        (my_outer >= 1, {"col": my_col - inner}),
        (my_inner + 1 < inner, {"col": my_col + 1}),
        (my_inner >= 1, {"col": my_col - 1}),
    )
    met = jnp.int32(rows - 1 + layers - 1)
    for there, device in lines:
        met = met + there.astype(jnp.int32)

        @pl.when(there)
        def _(device=device):
            pl.semaphore_signal(barrier, inc=1, device_id=device, device_id_type=MESH)

    row_peers = [lax.rem(my_row + d, rows) for d in range(1, rows)]
    layer_peers = [lax.rem(my_layer + d, layers) for d in range(1, layers)]
    for peer in row_peers:
        pl.semaphore_signal(barrier, inc=1, device_id={"row": peer}, device_id_type=MESH)
    for peer in layer_peers:
        pl.semaphore_signal(barrier, inc=1, device_id={"layer": peer}, device_id_type=MESH)
    pl.semaphore_wait(barrier, met)

    ending = []

    def send_left(kind, part, item, way, condition):
        def make():
            place = left_ref.at[item, part, panels]
            return pltpu.make_async_remote_copy(
                src_ref=place,
                dst_ref=place,
                send_sem=send_sem.at[kind, item, way],
                recv_sem=recv_sem.at[kind, item],
                device_id=lines[way][1],
                device_id_type=MESH,
            )

        condition = jnp.logical_and(condition, lines[way][0])

        @pl.when(condition)
        def _():
            make().start()

        ending.append((condition, make))

    def wait_left(kind, part, item, condition):
        @pl.when(condition)
        def _():
            place = left_ref.at[item, part, panels]
            pltpu.make_async_remote_copy(
                src_ref=place,
                dst_ref=place,
                send_sem=send_sem.at[kind, item, 0],
                recv_sem=recv_sem.at[kind, item],
                device_id={"col": my_col},
                device_id_type=MESH,
            ).wait_recv()

    always = my_col >= 0
    axes = (
        (outer, inner, my_outer, (0, 1)),
        (inner, 1, my_inner, (2, 3)),
    )

    def stages(kind, part, first, second):
        size1, stride1, me1, ways1 = first
        size2, stride2, me2, ways2 = second

        def own():
            for way in ways1 + ways2:
                send_left(kind, part, my_col, way, always)

        def along_first(step):
            for sign, way in ((-1, ways1[0]), (1, ways1[1])):
                at = me1 + sign * step
                there = at >= 0 if sign < 0 else at < size1
                item = at * stride1 + me2 * stride2
                wait_left(kind, part, item, there)
                for onward in (way,) + ways2:
                    send_left(kind, part, item, onward, there)

        def along_second(step):
            for sign, way in ((-1, ways2[0]), (1, ways2[1])):
                at = me2 + sign * step
                there = at >= 0 if sign < 0 else at < size2
                for other in range(size1):
                    item = other * stride1 + at * stride2
                    wait_left(kind, part, item, there)
                    send_left(kind, part, item, way, there)

        return (
            [own]
            + [functools.partial(along_first, s) for s in range(1, size1)]
            + [functools.partial(along_second, s) for s in range(1, size2)]
        )

    plans = [
        stages(kind, pl.ds(start, size), *(axes if straight else axes[::-1]))
        for kind, (start, size, straight) in enumerate(parts)
    ]

    def row_copy(d, peer):
        return pltpu.make_async_remote_copy(
            src_ref=right_ref.at[my_group, :, panels],
            dst_ref=right_ref.at[my_group, :, panels],
            send_sem=row_send.at[d],
            recv_sem=table_recv.at[my_group],
            device_id={"row": peer},
            device_id_type=MESH,
        )

    def layer_copy(d, peer, row):
        group = row * layers + my_layer
        return pltpu.make_async_remote_copy(
            src_ref=right_ref.at[group, :, panels],
            dst_ref=right_ref.at[group, :, panels],
            send_sem=layer_send.at[d, row],
            recv_sem=table_recv.at[group],
            device_id={"layer": peer},
            device_id_type=MESH,
        )

    def wait_table(group):
        pltpu.make_async_remote_copy(
            src_ref=right_ref.at[group, :, panels],
            dst_ref=right_ref.at[group, :, panels],
            send_sem=row_send.at[0],
            recv_sem=table_recv.at[group],
            device_id={"row": my_row},
            device_id_type=MESH,
        ).wait_recv()

    for plan in plans:
        plan[0]()
    for d, peer in enumerate(row_peers):
        row_copy(d, peer).start()
    for d, peer in enumerate(layer_peers):
        layer_copy(d, peer, my_row).start()
    for index in range(1, len(plans[0])):
        for plan in plans:
            plan[index]()
        if index == 1:
            for peer in row_peers:
                wait_table(peer * layers + my_layer)
                for d, layer_peer in enumerate(layer_peers):
                    layer_copy(d, layer_peer, peer).start()
    for layer_peer in layer_peers:
        for row in range(rows):
            wait_table(row * layers + layer_peer)
    for condition, make in ending:

        @pl.when(condition)
        def _(make=make):
            make().wait_send()

    for d, peer in enumerate(row_peers):
        row_copy(d, peer).wait_send()
    for d, peer in enumerate(layer_peers):
        for row in [my_row] + row_peers:
            layer_copy(d, peer, row).wait_send()


def spread(left, right, rows, cols, layers, half, halves):
    outer = 4 if cols % 4 == 0 else 1
    height = left.shape[1]
    swapped = max(height * 10 // 64, 1)
    chunk = left.shape[2] // halves
    panels = pl.ds(half * chunk, chunk)
    count = min(4, height - swapped)
    cuts = [swapped + (height - swapped) * k // count for k in range(count + 1)]
    parts = [(0, swapped, False)]
    parts += [(lo, hi - lo, True) for lo, hi in zip(cuts, cuts[1:])]
    kinds = len(parts)
    return pl.pallas_call(
        functools.partial(spread_kernel, rows, cols, layers, outer, tuple(parts), panels),
        out_shape=(
            jax.ShapeDtypeStruct(left.shape, left.dtype),
            jax.ShapeDtypeStruct(right.shape, right.dtype),
        ),
        in_specs=[pl.BlockSpec(memory_space=pl.ANY), pl.BlockSpec(memory_space=pl.ANY)],
        out_specs=(pl.BlockSpec(memory_space=pl.ANY), pl.BlockSpec(memory_space=pl.ANY)),
        input_output_aliases={0: 0, 1: 1},
        scratch_shapes=[
            pltpu.SemaphoreType.DMA((kinds, cols, 4)),
            pltpu.SemaphoreType.DMA((kinds, cols)),
            pltpu.SemaphoreType.DMA((rows,)),
            pltpu.SemaphoreType.DMA((layers, rows)),
            pltpu.SemaphoreType.DMA((rows * layers,)),
        ],
        compiler_params=pltpu.CompilerParams(collective_id=half, has_side_effects=True),
        cost_estimate=pl.CostEstimate(
            flops=0, bytes_accessed=1 << 30, transcendentals=0
        ),
        name="spread",
    )(left, right)


def multiply_kernel(pair_ref, turns_ref, left_ref, right_hbm, out_ref, table, sem):
    row = pl.program_id(0)
    nb = right_hbm.shape[0]
    width = out_ref.shape[1]
    panels = left_ref.shape[0] * left_ref.shape[2]

    @pl.when(row == 0)
    def _():
        copy = pltpu.make_async_copy(right_hbm, table.at[pl.ds(0, nb)], sem)
        copy.start()
        table[nb] = jnp.zeros_like(table[nb])
        copy.wait()

    group = 2 if width % 2 == 0 else 1
    for base in range(0, width, group):

        def step(turn, sums, base=base):
            new = []
            for j in range(group):
                start = (row * width + base + j) * panels + turn * QUAD
                lefts, rights = [], []
                for q in range(QUAD):
                    code = pair_ref[start + q]
                    panel, place = code // 1024, lax.rem(code, 1024)
                    lefts.append(left_ref[panel // width, 0, lax.rem(panel, width)])
                    rights.append(table[place, base + j])
                new.append(
                    sums[j]
                    + jnp.dot(
                        jnp.concatenate(lefts, axis=1),
                        jnp.concatenate(rights, axis=0),
                        preferred_element_type=jnp.float32,
                    )
                )
            return tuple(new)

        zero = jnp.zeros(out_ref.shape[2:], jnp.float32)
        turns = turns_ref[row * width + base]
        for j in range(1, group):
            turns = jnp.maximum(turns, turns_ref[row * width + base + j])
        sums = lax.fori_loop(0, turns, step, (zero,) * group)
        for j in range(group):
            out_ref[0, base + j] = sums[j].astype(out_ref.dtype)


def multiply(pairs, turns, left, right):
    cols, height, width, size, _ = left.shape
    nb = right.shape[0]
    table_bytes = (nb + 1) * width * size * size * 2
    return pl.pallas_call(
        multiply_kernel,
        out_shape=jax.ShapeDtypeStruct((height, width, size, size), left.dtype),
        grid_spec=pltpu.PrefetchScalarGridSpec(
            num_scalar_prefetch=2,
            grid=(height,),
            in_specs=[
                pl.BlockSpec((cols, 1, width, size, size), lambda i, *_: (0, i, 0, 0, 0)),
                pl.BlockSpec(memory_space=pl.ANY),
            ],
            out_specs=pl.BlockSpec((1, width, size, size), lambda i, *_: (i, 0, 0, 0)),
            scratch_shapes=[
                pltpu.VMEM((nb + 1, width, size, size), left.dtype),
                pltpu.SemaphoreType.DMA,
            ],
        ),
        compiler_params=pltpu.CompilerParams(vmem_limit_bytes=table_bytes + (10 << 20)),
        name="multiply",
    )(pairs, turns, left, right)


def shards(owned_blocks, slot_rows, block_cols):
    own_slots, panels, size, _ = owned_blocks.shape
    rows = lax.axis_size("row")
    cols = lax.axis_size("col")
    layers = lax.axis_size("layer")
    width = panels // cols
    slots = own_slots * rows * cols * layers
    my_row, my_col, my_layer = (lax.axis_index(a) for a in ("row", "col", "layer"))
    my_group = my_row * layers + my_layer

    ids = jnp.concatenate([slot_rows[:, None], block_cols], axis=1)
    ids = lax.all_gather(ids, ("row", "col", "layer"), axis=0, tiled=True)
    nb = NB
    per_layer = panels // (cols * layers) * (nb // panels)
    height = nb // (rows * layers)
    place = jnp.arange(nb, dtype=jnp.int32)
    part, within = place // height, place % height
    row_at = (
        part // layers * (nb // rows)
        + within // per_layer * per_layer * layers
        + part % layers * per_layer
        + within % per_layer
    )
    holds = ids[None, :, 0] == row_at[:, None]
    slot_at = jnp.sum(
        jnp.where(holds, jnp.arange(slots, dtype=jnp.int32)[None, :], 0), axis=1
    )
    my_slots = lax.dynamic_slice_in_dim(slot_at, my_group * height, height)
    owner = my_slots // own_slots // layers % cols
    index = owner * own_slots + my_slots % own_slots
    spot = jnp.stack([my_col, my_group]).astype(jnp.int32)
    shapes = (
        jax.ShapeDtypeStruct((cols, height, width, size, size), owned_blocks.dtype),
        jax.ShapeDtypeStruct((rows * layers, height, width, size, size), owned_blocks.dtype),
    )
    halves = 2 if width % 2 == 0 else 1
    chunk = width // halves
    owned = owned_blocks.reshape(own_slots, cols, width, size, size)
    owned, ids = lax.optimization_barrier((owned, ids))
    arrived = []
    for half in range(halves):
        piece = owned[:, :, half * chunk:(half + 1) * chunk]
        if arrived:
            piece, arrived[-1] = lax.optimization_barrier((piece, arrived[-1]))
        got = lax.all_to_all(piece, "col", split_axis=1, concat_axis=0, tiled=True)
        arrived.append(got.reshape(cols * own_slots, chunk, size, size))
    tables = ()
    for half in range(halves):
        tables = pick_rows(index, spot, arrived[half], shapes, half, tables)
        tables = spread(*tables, rows, cols, layers, half, halves)
    left, right = tables

    columns = jnp.dot(
        holds.astype(jnp.float32),
        ids[:, 1:].astype(jnp.float32),
        precision=lax.Precision.HIGHEST,
    ).astype(jnp.int32)
    mine = lax.dynamic_slice_in_dim(columns, my_group * height, height)
    wanted = lax.dynamic_slice_in_dim(mine, my_col * width, width, 1)
    inside = mine % (nb // rows)
    partner = (
        (mine // (nb // rows) * layers + inside // per_layer % layers) * height
        + inside // (per_layer * layers) * per_layer
        + inside % per_layer
    )
    reach = lax.dynamic_slice_in_dim(columns, my_col * width, width, 1)
    matched = reach[partner] == wanted[:, None, :]
    matched = matched.transpose(0, 2, 1)
    order = jnp.cumsum(matched.astype(jnp.int32), axis=2) - 1
    code = jnp.arange(panels, dtype=jnp.int32)[None, :] * 1024 + partner
    lane = jnp.arange(panels, dtype=jnp.int32)
    taken = matched[..., None] & (order[..., None] == lane)
    pairs = jnp.sum(jnp.where(taken, (code - nb)[:, None, :, None], 0), axis=2) + nb
    turns = (jnp.sum(matched, axis=2, dtype=jnp.int32) + QUAD - 1) // QUAD
    return multiply(
        pairs.reshape(-1), turns.reshape(-1), left, right.reshape(nb, width, size, size)
    )


NB = 256


def solution(mesh):
    return jax.shard_map(
        shards,
        mesh=mesh,
        in_specs=(
            P(("row", "col", "layer"), None, None, None),
            P(("row", "col", "layer")),
            P(("row", "col", "layer"), None),
        ),
        out_specs=P(("row", "layer"), "col", None, None),
        check_vma=False,
    )
```
